32 devices in a mesh: row: 8 (over z, x), col: 4 (over y, core).
Axes of the slice: x: 2, y: 2, z: 4, core: 2. Of those that a mesh axis runs over, the one named last changes fastest.
Arguments:
- geneo_vectors: bfloat16 [32, 32, 512, 512], P(None, None, 'row', 'col'), as said below
- phase_labels: int32 [32, 512, 512], P(None, 'row', 'col'), may hold values from 0 to 3, as said below
- phase_mobility: float32 [4], replicated, may hold values from 0.5 to 5
Outputs:
- coarse_factor: float32 [32, 4, 4, 2, 2, 8, 2, 32], P(None, None, 'col', None, None, 'row')
The draws below stay inside these ranges and needn't reach their ends.
Inputs may be any that keep to these rules, and one draw needn't show every extreme that they name: `geneo_vectors`: the 32 vectors of each subdomain are linearly independent on its cells. `phase_labels`: within one subdomain the labels take one or two values, some q and (q + 1) modulo 4.
All inputs are finite; a program needn't handle non-finite values.
Results may differ from the reference program's by a relative error of at most 0.00055.
Values may be sent and summed in bfloat16 or wider, within the bound.
A program may use at most 512 MiB of HBM per device.

```python
import math
import jax
import jax.numpy as jnp
from jax import lax

K = 32
NB = 2
PHASES = 4
CX = 64
CY = 128
CZ = 32
NX = 512
NY = 512
NSUB = 32
ORDER = 1024
KTR = 2
KTC = 4
WIDTH = 64
N_ROW = 8
N_COL = 4


def smooth_line(key, count, length):
    key_amp, key_wave, key_shift = jax.random.split(key, 3)
    amplitude = jnp.clip(jax.random.normal(key_amp, (count, 4, 1), jnp.float32), -3.0, 3.0) * 0.7071
    wavenumber = jax.random.uniform(key_wave, (count, 4, 1), jnp.float32, 0.0, 0.6)
    offset = jax.random.uniform(key_shift, (count, 4, 1), jnp.float32, -3.1416, 3.1416)
    coords = jnp.arange(length, dtype=jnp.float32)[None, None, :]
    values = amplitude * jnp.cos(wavenumber * coords + offset)
    return values[:, 0] + values[:, 1] + values[:, 2] + values[:, 3]


def draw_geneo_vectors(key, part):
    key_line, key_own, key_mix, key_noise = jax.random.split(key, 4)
    terms = 3
    line_x = smooth_line(jax.random.fold_in(key_line, 0), K * terms, NX).reshape(K, terms, NX)
    line_y = smooth_line(jax.random.fold_in(key_line, 1), K * terms, NY).reshape(K, terms, NY)
    line_z = smooth_line(jax.random.fold_in(key_line, 2), K * terms, CZ).reshape(K, terms, CZ)
    blocks_x = NX // CX
    blocks_y = NY // CY
    own_low, own_high, mix_bound = (0.6, 1.4, 0.5)
    own_scale = jax.random.uniform(key_own, (K, blocks_x, blocks_y), jnp.float32, own_low, own_high)
    mixing = jax.random.uniform(key_mix, (3, K, blocks_x, blocks_y), jnp.float32, -mix_bound, mix_bound)
    steps_list = (1, 5, 11)

    def expand(grid):
        return jnp.repeat(jnp.repeat(grid, CX, axis=0), CY, axis=1)

    def base_of(vector):
        total = jnp.zeros((CZ, NX, NY), jnp.float32)
        for term in range(terms):
            total = total + line_z[vector, term][:, None, None] * line_x[vector, term][None, :, None] * line_y[vector, term][None, None, :]
        return total * 0.57735
    coords_x = jnp.arange(NX) % CX
    coords_y = jnp.arange(NY) % CY
    dist_x = jnp.minimum(coords_x, CX - 1 - coords_x)
    dist_y = jnp.minimum(coords_y, CY - 1 - coords_y)
    dist = jnp.minimum(dist_x[:, None], dist_y[None, :]).astype(jnp.float32)
    envelope = 1.0 + 4.0 * jnp.exp(-dist)

    def one_vector(vector):
        mixed = expand(own_scale[vector])[None, :, :] * base_of(vector)
        for index, step in enumerate(steps_list):
            mixed = mixed + expand(mixing[index, vector])[None, :, :] * base_of((vector + step) % K)
        noise_key = jax.random.fold_in(key_noise, vector)
        noise = jnp.clip(jax.random.normal(noise_key, (CZ, NX, NY), jnp.float32), -4.0, 4.0)
        return mixed * envelope[None, :, :] + 0.12 * noise
    factor = 0.5 * float(CX * CY * CZ) ** (-0.5)
    fields = lax.map(one_vector, jnp.arange(K, dtype=jnp.int32))
    return (fields * factor).astype(jnp.bfloat16)


def draw_phase_labels(key, part):
    key_cell, key_zone = jax.random.split(key)
    cells = jax.random.randint(key_cell, (CZ, NX, NY), 0, 2)
    zones = jax.random.randint(key_zone, (1, NX // CX, NY // CY), 0, PHASES)
    zones = jnp.repeat(jnp.repeat(zones, CX, axis=1), CY, axis=2)
    return ((cells + zones) % PHASES).astype(jnp.int32)


def setup_inputs(seed: int = 0) -> dict:
    key_of = jax.random.split(jax.random.key(seed), 4)
    return {
        "geneo_vectors": draw_geneo_vectors(jax.random.fold_in(key_of[3], 71), 0),
        "phase_labels": draw_phase_labels(jax.random.fold_in(key_of[3], 71), 0),
        "phase_mobility": jnp.clip(jnp.exp(jax.random.uniform(key_of[2], (PHASES,), jnp.float32, math.log(0.5), math.log(5.0))), 0.5, 5.0),
    }


FACES = ((-1, 0), (1, 0), (0, -1), (0, 1))

def slot_offsets():
    offsets = [((0, 0), (0, 0))]
    for face in FACES:
        offsets += [((0, 0), face), (face, (0, 0)), (face, face)]
    for face_x in FACES[:2]:
        for face_y in FACES[2:]:
            offsets += [(face_x, face_y), (face_y, face_x)]
    return offsets

def band_index(from_off, to_off):
    return (to_off[0] - from_off[0] + 1) * 3 + (to_off[1] - from_off[1] + 1)

def laplace_own(own):
    field = own.astype(jnp.float32)
    padded = jnp.pad(field, ((0, 0), (1, 1), (1, 1), (1, 1)))
    near = padded[:, 2:, 1:-1, 1:-1] + padded[:, :-2, 1:-1, 1:-1]
    near = near + padded[:, 1:-1, 2:, 1:-1] + padded[:, 1:-1, :-2, 1:-1]
    near = near + padded[:, 1:-1, 1:-1, 2:] + padded[:, 1:-1, 1:-1, :-2]
    return near - 6.0 * field

def contract_cells(left, right):
    flat_left = left.reshape(left.shape[0], -1)
    flat_right = right.reshape(right.shape[0], -1)
    return lax.dot_general(flat_left.astype(jnp.float32), flat_right.astype(jnp.float32), (((1,), (1,)), ((), ())), preferred_element_type=jnp.float32)

def local_tiles(window, labels, mobility_table):
    own = window[:, :, 1:-1, 1:-1]
    root_table = jnp.sqrt(mobility_table)
    cell_root = jnp.zeros(labels.shape, jnp.float32)
    for phase in range(mobility_table.shape[0]):
        cell_root = cell_root + jnp.where(labels == phase, root_table[phase], jnp.float32(0.0))
    flux = (laplace_own(own) * cell_root).astype(jnp.bfloat16)
    tiles = [contract_cells(own, own) + contract_cells(flux, flux)]
    face_data = [(flux[:, :, 0, :], window[:, :, 0, 1:-1], cell_root[:, 0, :]), (flux[:, :, -1, :], window[:, :, -1, 1:-1], cell_root[:, -1, :]), (flux[:, :, :, 0], window[:, :, 1:-1, 0], cell_root[:, :, 0]), (flux[:, :, :, -1], window[:, :, 1:-1, -1], cell_root[:, :, -1])]
    for layer_f, layer_z, layer_r in face_data:
        across = (layer_z.astype(jnp.float32) * layer_r).astype(jnp.bfloat16)
        cross = contract_cells(layer_f, across)
        tiles += [cross, cross.T, contract_cells(across, across)]
    for x_first in (True, False):
        for y_first in (True, False):
            inner_x = 1 if x_first else -2
            outer_x = 0 if x_first else -1
            inner_y = 1 if y_first else -2
            outer_y = 0 if y_first else -1
            cell_x = 0 if x_first else -1
            cell_y = 0 if y_first else -1
            corner_r = cell_root[:, cell_x, cell_y]
            along_x = (window[:, :, outer_x, inner_y].astype(jnp.float32) * corner_r).astype(jnp.bfloat16)
            along_y = (window[:, :, inner_x, outer_y].astype(jnp.float32) * corner_r).astype(jnp.bfloat16)
            pair = contract_cells(along_x, along_y)
            tiles += [pair, pair.T]
    return jnp.stack(tiles)

def shift_grid(values, offset):
    widths = [(1, 1), (1, 1)] + [(0, 0)] * (values.ndim - 2)
    padded = jnp.pad(values, widths)
    start_x = 1 - offset[0]
    start_y = 1 - offset[1]
    return padded[start_x:start_x + values.shape[0], start_y:start_y + values.shape[1]]

def reference(geneo_vectors, phase_labels, phase_mobility):
    padded = jnp.pad(geneo_vectors, ((0, 0), (0, 0), (1, 1), (1, 1)))
    zero = jnp.zeros((), jnp.int32)

    def one_device(index):
        grid_x = (index // N_COL).astype(jnp.int32)
        grid_y = (index % N_COL).astype(jnp.int32)
        start_x = (grid_x * CX).astype(jnp.int32)
        start_y = (grid_y * CY).astype(jnp.int32)
        window = lax.dynamic_slice(padded, (zero, zero, start_x, start_y), (K, CZ, CX + 2, CY + 2))
        labels = lax.dynamic_slice(phase_labels, (zero, start_x, start_y), (CZ, CX, CY))
        return local_tiles(window, labels, phase_mobility)
    offsets = slot_offsets()
    tiles = lax.map(one_device, jnp.arange(NSUB, dtype=jnp.int32))
    grid = tiles.reshape(N_ROW, N_COL, len(offsets), K, K)
    bands = [jnp.zeros((N_ROW, N_COL, K, K), jnp.float32) for count in range(9)]
    for slot, pair_off in enumerate(offsets):
        place = band_index(pair_off[0], pair_off[1])
        bands[place] = bands[place] + shift_grid(grid[:, :, slot], pair_off[0])
    sub_x = (jnp.arange(NSUB, dtype=jnp.int32) // N_COL).astype(jnp.int32)
    sub_y = (jnp.arange(NSUB, dtype=jnp.int32) % N_COL).astype(jnp.int32)
    dense = jnp.zeros((NSUB, K, NSUB, K), jnp.float32)
    for index in range(9):
        step_x = index // 3 - 1
        step_y = index % 3 - 1
        match = ((sub_x[None, :] == sub_x[:, None] + step_x) & (sub_y[None, :] == sub_y[:, None] + step_y)).astype(jnp.float32)
        dense = dense + match[:, None, :, None] * bands[index].reshape(NSUB, K, 1, K)
    matrix = dense.reshape(ORDER, ORDER)
    for panel in range(2):
        first = panel * WIDTH
        last = first + WIDTH
        low = jnp.linalg.cholesky(matrix[first:last, first:last])
        block = matrix[first:, first:last].T
        solved = lax.linalg.triangular_solve(low, block, left_side=True, lower=True)
        matrix = matrix.at[:first, first:last].set(0.0)
        matrix = matrix.at[first:, first:last].set(solved.T)
        tail = solved[:, WIDTH:]
        product = lax.dot_general(tail.astype(jnp.float32), tail.astype(jnp.float32), (((0,), (0,)), ((), ())), precision=lax.Precision.HIGHEST, preferred_element_type=jnp.float32)
        matrix = matrix.at[last:, last:].add(-product)
        matrix = matrix.at[first:last, last:].set(0.0)
    shaped = matrix.reshape(NSUB, KTR, N_ROW, NB, NSUB, KTC, N_COL, NB)
    return shaped.transpose(4, 5, 6, 7, 1, 2, 3, 0)
```

```python
import jax
import jax.numpy as jnp
from jax import lax
from jax.experimental import pallas as pl
from jax.experimental.pallas import tpu as pltpu
from jax.sharding import PartitionSpec as P

NB = 2
PSUB = 2


FACES = ((-1, 0), (1, 0), (0, -1), (0, 1))


def with_halo(cells, sides, width):
    for axis, dim in sides:
        count = lax.axis_size(axis)
        ends = count - 1
        head = lax.slice_in_dim(cells, 0, width, axis=dim)
        tail = lax.slice_in_dim(cells, cells.shape[dim] - width, cells.shape[dim], axis=dim)
        cells = jnp.concatenate(
            [
                lax.ppermute(tail, axis, [(i, (i + 1) % count) for i in range(ends)]),
                cells,
                lax.ppermute(head, axis, [((i + 1) % count, i) for i in range(ends)]),
            ],
            axis=dim,
        )
    return cells


def slot_offsets():
    offsets = [((0, 0), (0, 0))]
    for face in FACES:
        offsets += [((0, 0), face), (face, (0, 0)), (face, face)]
    for face_x in FACES[:2]:
        for face_y in FACES[2:]:
            offsets += [(face_x, face_y), (face_y, face_x)]
    return offsets


def band_index(from_off, to_off):
    return (to_off[0] - from_off[0] + 1) * 3 + (to_off[1] - from_off[1] + 1)


def from_next(field, axis):
    count = field.shape[axis]
    inner = lax.slice_in_dim(field, 1, count, axis=axis)
    blank = jnp.zeros_like(lax.slice_in_dim(field, 0, 1, axis=axis))
    return jnp.concatenate([inner, blank], axis=axis)


def from_prev(field, axis):
    count = field.shape[axis]
    inner = lax.slice_in_dim(field, 0, count - 1, axis=axis)
    blank = jnp.zeros_like(lax.slice_in_dim(field, 0, 1, axis=axis))
    return jnp.concatenate([blank, inner], axis=axis)


def laplace_own(own):
    field = own.astype(jnp.float32)
    near = from_next(field, 1) + from_prev(field, 1)
    near = near + from_next(field, 2) + from_prev(field, 2)
    near = near + from_next(field, 3) + from_prev(field, 3)
    return near - 6.0 * field


def contract_cells(left, right):
    flat_left = left.reshape(left.shape[0], -1)
    flat_right = right.reshape(right.shape[0], -1)
    return lax.dot_general(
        flat_left, flat_right, (((1,), (1,)), ((), ())), preferred_element_type=jnp.float32
    )


SUBL = 16


def flux_gram_kernel(prev_ref, cur_ref, next_ref, root_ref, acc_ref, fx_ref, edge_ref, flux_ref):
    z = pl.program_id(0)
    n_z = pl.num_programs(0)
    vectors, n_x, n_y = flux_ref.shape
    half = n_y // 2

    @pl.when(z == 0)
    def _():
        acc_ref[...] = jnp.zeros_like(acc_ref)
        edge_ref[...] = jnp.zeros_like(edge_ref)

    use_prev = (z > 0).astype(jnp.float32)
    use_next = (z < n_z - 1).astype(jnp.float32)

    def step(v, carry):
        rows = lax.broadcasted_iota(jnp.int32, (n_x, n_y), 0)
        lanes = lax.broadcasted_iota(jnp.int32, (n_x, n_y), 1)
        own = cur_ref[v, 0].astype(jnp.float32)
        near = next_ref[v, 0].astype(jnp.float32) * use_next
        near = near + prev_ref[v, 0].astype(jnp.float32) * use_prev
        near = near + jnp.where(rows == n_x - 1, 0.0, pltpu.roll(own, n_x - 1, 0))
        near = near + jnp.where(rows == 0, 0.0, pltpu.roll(own, 1, 0))
        near = near + jnp.where(lanes == n_y - 1, 0.0, pltpu.roll(own, n_y - 1, 1))
        near = near + jnp.where(lanes == 0, 0.0, pltpu.roll(own, 1, 1))
        flux = ((near - 6.0 * own) * root_ref[0]).astype(jnp.bfloat16)
        flux_ref[v] = flux
        wide = flux.astype(jnp.float32)
        fx_ref[v, 0, 0:1, :] = wide[0:1, :]
        fx_ref[v, 0, 1:2, :] = wide[n_x - 1 : n_x, :]
        turned_f = pltpu.roll(wide, 2 * z + 1, 1)
        turned_o = pltpu.roll(own, 2 * z + 1 + half, 1)
        kept = edge_ref[v]
        is_f = (lanes >= 2 * z) & (lanes < 2 * z + 2)
        is_o = (lanes >= 2 * z + half) & (lanes < 2 * z + 2 + half)
        edge_ref[v] = jnp.where(is_f, turned_f, jnp.where(is_o, turned_o, kept))
        return carry

    lax.fori_loop(0, vectors, step, 0)
    for block in range(n_x // SUBL):
        span = slice(block * SUBL, (block + 1) * SUBL)
        left = cur_ref[:, 0, span, :].reshape(vectors * SUBL, n_y)
        right = flux_ref[:, span, :].reshape(vectors * SUBL, n_y)
        both = jnp.concatenate([left, right], axis=1)
        acc_ref[...] += lax.dot_general(
            both, both, (((1,), (1,)), ((), ())), preferred_element_type=jnp.float32
        )


def flux_gram(own, cell_root):
    vectors, n_z, n_x, n_y = own.shape
    order = vectors * SUBL
    block = (vectors, 1, n_x, n_y)
    acc, flux_x, edges = pl.pallas_call(
        flux_gram_kernel,
        grid=(n_z,),
        in_specs=[
            pl.BlockSpec(block, lambda z: (0, jnp.maximum(z - 1, 0), 0, 0)),
            pl.BlockSpec(block, lambda z: (0, z, 0, 0)),
            pl.BlockSpec(block, lambda z: (0, jnp.minimum(z + 1, n_z - 1), 0, 0)),
            pl.BlockSpec((1, n_x, n_y), lambda z: (z, 0, 0)),
        ],
        out_specs=[
            pl.BlockSpec((order, order), lambda z: (0, 0)),
            pl.BlockSpec((vectors, 1, 2, n_y), lambda z: (0, z, 0, 0)),
            pl.BlockSpec((vectors, n_x, n_y), lambda z: (0, 0, 0)),
        ],
        out_shape=[
            jax.ShapeDtypeStruct((order, order), jnp.float32),
            jax.ShapeDtypeStruct((vectors, n_z, 2, n_y), jnp.float32),
            jax.ShapeDtypeStruct((vectors, n_x, n_y), jnp.float32),
        ],
        scratch_shapes=[pltpu.VMEM((vectors, n_x, n_y), jnp.bfloat16)],
        compiler_params=pltpu.CompilerParams(vmem_limit_bytes=40 * 1024 * 1024),
    )(own, own, own, cell_root)
    place = jnp.arange(order, dtype=jnp.int32) % SUBL
    acc = jnp.where(place[:, None] == place[None, :], acc, jnp.float32(0.0))
    half_sum = acc.reshape(vectors, SUBL, order).sum(1)
    gram = half_sum.reshape(vectors, vectors, SUBL).sum(2)
    half = n_y // 2
    edges = edges.astype(jnp.bfloat16)
    flux_edge = edges[:, :, : 2 * n_z].reshape(vectors, n_x, n_z, 2)
    own_edge = edges[:, :, half : half + 2 * n_z].reshape(vectors, n_x, n_z, 2)
    return gram, flux_x.astype(jnp.bfloat16), flux_edge, own_edge


def local_tiles(own, labels, mobility_table):
    rims_x = jnp.stack([own[:, :, 0, :], own[:, :, -1, :]], axis=2)
    wide_x = with_halo(rims_x, (("row", 2),), 1)
    lower_x = wide_x[:, :, 0, :]
    upper_x = wide_x[:, :, 3, :]
    root_table = jnp.sqrt(mobility_table)
    cell_root = jnp.zeros(labels.shape, jnp.float32)
    for phase in range(mobility_table.shape[0]):
        cell_root = cell_root + jnp.where(labels == phase, root_table[phase], jnp.float32(0.0))
    gram, flux_x, flux_edge, own_edge = flux_gram(own, cell_root)
    tiles = [gram]
    count = lax.axis_size("col")
    lower_y = lax.ppermute(own_edge[..., 0], "col", [(i, i + 1) for i in range(count - 1)])
    upper_y = lax.ppermute(own_edge[..., 1], "col", [(i + 1, i) for i in range(count - 1)])
    face_data = [
        (flux_x[:, :, 0, :], lower_x, cell_root[:, 0, :]),
        (flux_x[:, :, 1, :], upper_x, cell_root[:, -1, :]),
        (flux_edge[..., 1], lower_y, cell_root[:, :, 0].T),
        (flux_edge[..., 0], upper_y, cell_root[:, :, -1].T),
    ]
    for layer_f, layer_z, layer_r in face_data:
        across = (layer_z.astype(jnp.float32) * layer_r).astype(jnp.bfloat16)
        cross = contract_cells(layer_f, across)
        tiles += [cross, cross.T, contract_cells(across, across)]
    for x_first in (True, False):
        for y_first in (True, False):
            layer_x = lower_x if x_first else upper_x
            layer_y = lower_y if y_first else upper_y
            cell_x = 0 if x_first else -1
            cell_y = 0 if y_first else -1
            corner_r = cell_root[:, cell_x, cell_y]
            along_x = (layer_x[:, :, cell_y].astype(jnp.float32) * corner_r).astype(jnp.bfloat16)
            along_y = (layer_y[:, cell_x, :].astype(jnp.float32) * corner_r).astype(jnp.bfloat16)
            pair = contract_cells(along_x, along_y)
            tiles += [pair, pair.T]
    return jnp.stack(tiles)


def shift_grid(values, offset):
    widths = [(1, 1), (1, 1)] + [(0, 0)] * (values.ndim - 2)
    padded = jnp.pad(values, widths)
    start_x = 1 - offset[0]
    start_y = 1 - offset[1]
    return padded[start_x : start_x + values.shape[0], start_y : start_y + values.shape[1]]


def to_owner(stack, n_row, n_col):
    slots = stack.shape[0]
    vectors = stack.shape[1]
    row_blocks = vectors // (NB * n_row)
    col_blocks = vectors // (NB * n_col)
    split = stack.reshape(slots, row_blocks, n_row, NB, col_blocks, n_col, NB)
    moved = split.transpose(2, 5, 0, 4, 6, 1, 3)
    return moved.reshape(n_row, n_col, slots * col_blocks * NB * row_blocks * NB)


def place_bands(bands, n_row, n_col):
    n_sub = n_row * n_col
    sub_x = jnp.arange(n_sub, dtype=jnp.int32) // n_col
    sub_y = jnp.arange(n_sub, dtype=jnp.int32) % n_col
    total = None
    for index in range(9):
        step_x = index // 3 - 1
        step_y = index % 3 - 1
        match = (
            (sub_x[:, None] == sub_x[None, :] + step_x)
            & (sub_y[:, None] == sub_y[None, :] + step_y)
        ).astype(jnp.float32)
        flat = bands[index].reshape(n_sub, -1).T
        term = match[:, None, :] * flat[None, :, :]
        total = term if total is None else total + term
    return total


def body(geneo_vectors, phase_labels, phase_mobility):
    vectors = geneo_vectors.shape[0]
    n_row = lax.axis_size("row")
    n_col = lax.axis_size("col")
    n_sub = n_row * n_col
    row_blocks = vectors // (NB * n_row)
    col_blocks = vectors // (NB * n_col)
    rows_here = row_blocks * NB * n_sub
    piece_len = col_blocks * NB * row_blocks * NB
    width = PSUB * vectors
    tiles = local_tiles(geneo_vectors, phase_labels, phase_mobility)
    offsets = slot_offsets()
    routed = lax.all_to_all(
        lax.all_to_all(
            to_owner(tiles, n_row, n_col), "row", split_axis=0, concat_axis=0, tiled=True
        ),
        "col",
        split_axis=1,
        concat_axis=1,
        tiled=True,
    )
    routed = routed.reshape(n_row, n_col, len(offsets), piece_len)
    bands = [jnp.zeros((n_row, n_col, piece_len), jnp.float32) for count in range(9)]
    for slot, pair_off in enumerate(offsets):
        place = band_index(pair_off[0], pair_off[1])
        bands[place] = bands[place] + shift_grid(routed[:, :, slot], pair_off[0])
    local = place_bands(bands, n_row, n_col).reshape(n_sub, col_blocks * NB, rows_here)
    row_index = lax.axis_index("row")
    col_index = lax.axis_index("col")
    row_sub = jnp.arange(rows_here, dtype=jnp.int32) % n_sub
    ends = 2 * PSUB
    mine = local[:ends].reshape(ends, col_blocks, NB, rows_here)
    parts = lax.all_gather(mine, ("row", "col"), axis=0, tiled=False)
    parts = parts.reshape(n_row, n_col, ends, col_blocks, NB, rows_here)
    panels = parts.transpose(2, 3, 1, 4, 0, 5).reshape(2, width, n_row, rows_here)

    def rows_of(block, first, last):
        grid = block.reshape(width, n_row, row_blocks, NB, n_sub)[..., first:last]
        return grid.transpose(0, 4, 2, 1, 3).reshape(width, (last - first) * vectors)

    done = []
    for panel in range(2):
        first = panel * PSUB
        last = first + PSUB
        block = panels[panel]
        for solved in done:
            change = lax.dot_general(
                rows_of(solved, first, last),
                solved.reshape(width, n_row * rows_here),
                (((0,), (0,)), ((), ())),
                precision=lax.Precision.HIGHEST,
                preferred_element_type=jnp.float32,
            )
            block = block - change.reshape(width, n_row, rows_here)
        block = jnp.where(row_sub >= first, block, jnp.float32(0.0))
        low = jnp.linalg.cholesky(rows_of(block, first, last).T)
        solved = lax.linalg.triangular_solve(
            low, block.reshape(width, n_row * rows_here), left_side=True, lower=True
        ).reshape(width, n_row, rows_here)
        done.append(solved)
    both = jnp.concatenate(done, axis=0)
    rows_mine = lax.dynamic_index_in_dim(both, row_index, 1, keepdims=False)
    by_block = both.reshape(2 * width, n_row, row_blocks, NB, n_sub).transpose(0, 2, 1, 3, 4)
    picked = lax.dynamic_index_in_dim(
        by_block.reshape(2 * width, row_blocks, n_row // n_col, n_col, NB, n_sub),
        col_index,
        3,
        keepdims=False,
    )
    columns = (
        picked.reshape(2 * width, col_blocks * NB, n_sub)
        .transpose(0, 2, 1)
        .reshape(2 * width, n_sub * col_blocks * NB)
    )
    update = lax.dot_general(
        columns,
        rows_mine,
        (((0,), (0,)), ((), ())),
        precision=lax.Precision.HIGHEST,
        preferred_element_type=jnp.float32,
    ).reshape(n_sub, col_blocks * NB, rows_here)
    panel_mine = lax.dynamic_index_in_dim(
        rows_mine.reshape(ends, col_blocks, n_col, NB, rows_here), col_index, 2, keepdims=False
    ).reshape(ends, col_blocks * NB, rows_here)
    rest = jnp.where(row_sub < ends, jnp.float32(0.0), local[ends:] - update[ends:])
    local = jnp.concatenate([panel_mine, rest], axis=0)
    return local.reshape(n_sub, col_blocks, 1, NB, row_blocks, 1, NB, n_sub)


def solution(mesh):
    return jax.shard_map(
        body,
        mesh=mesh,
        in_specs=(P(None, None, "row", "col"), P(None, "row", "col"), P()),
        out_specs=P(None, None, "col", None, None, "row", None, None),
        check_vma=False,
    )
```
